256 devices in a mesh: ctx: 16 (over y, x), dp: 16 (over z, core).
Axes of the slice: x: 4, y: 4, z: 8, core: 2. Of those that a mesh axis runs over, the one named last changes fastest.
Arguments:
- queries: bfloat16 [16, 4096, 4096], P('dp', 'ctx'), may hold values from -6 to 6
- key_states: bfloat16 [16, 4096, 512], P('dp', 'ctx'), may hold values from -6 to 6
- value_states: bfloat16 [16, 4096, 512], P('dp', 'ctx'), may hold values from -6 to 6
- targets: bfloat16 [16, 4096, 4096], P('dp', 'ctx'), may hold values from -32 to 32
- doc_blocks: int32 [16, 8], P('dp'), may hold values from 1 to 6, 32 in all within a row
- doc_domain: int32 [16, 8], P('dp'), may hold values from 0 to 21
- domain_weight: float32 [22], replicated, may hold values from 0.25 to 4
Outputs:
- grad_queries: bfloat16 [16, 4096, 4096], P('dp', 'ctx')
- grad_keys: bfloat16 [16, 4096, 512], P('dp', 'ctx')
- grad_values: bfloat16 [16, 4096, 512], P('dp', 'ctx')
- domain_loss: float32 [22], replicated
The draws below stay inside these ranges and needn't reach their ends.
Inputs may be any that keep to these rules, and one draw needn't show every extreme that they name: `doc_blocks`: A slab's documents take whole blocks of 128 rows, fill its 4096 rows exactly, and some document takes 6 blocks.
All inputs are finite; a program needn't handle non-finite values.
Results may differ from the reference program's by a relative error of at most 0.015.
Values may be sent and summed in bfloat16 or wider, within the bound.
A program may use at most 64 MiB of HBM per device.

```python
import math
import jax
import jax.numpy as jnp
import numpy as np
from jax import lax

HQ = 32
HK = 4
HD = 128
BLOCK = 128
MOST = 6
DOMAINS = 22
SLAB = 4096
DOCS = 8
N_DP = 16


def block_offsets(key):
    shape = (N_DP, SLAB // BLOCK, HK * HD)
    table = jnp.clip(1.2 * jax.random.normal(jax.random.fold_in(key, 22), shape, jnp.float32), -2.4, 2.4)
    return jnp.repeat(table, BLOCK, axis=1)


def head_scales(key):
    ranks = jax.random.permutation(jax.random.fold_in(key, 23), HQ).astype(jnp.float32)
    return 0.2 * jnp.power(10.0, ranks / max(HQ - 1, 1))


def draw_queries(key, part):
    shape = (N_DP, SLAB, HQ * HD)
    drawn = jnp.clip(jax.random.normal(jax.random.fold_in(key, 1), shape, jnp.float32), -6.0, 6.0)
    return drawn.astype(jnp.bfloat16)


def draw_key_states(key, part):
    shape = (N_DP, SLAB, HK * HD)
    drawn = jnp.clip(jax.random.normal(jax.random.fold_in(key, 3), shape, jnp.float32), -6.0, 6.0)
    return drawn.astype(jnp.bfloat16)


def draw_value_states(key, part):
    shape = (N_DP, SLAB, HK * HD)
    offsets = block_offsets(key)
    drawn = 0.7 * jnp.clip(jax.random.normal(jax.random.fold_in(key, 10), shape, jnp.float32), -3.0, 3.0)
    return (drawn + offsets).astype(jnp.bfloat16)


def draw_targets(key, part):
    group = HQ // HK
    shape = (N_DP, SLAB, HK, group, HD)
    slab_pos = jnp.arange(N_DP, dtype=jnp.float32)[:, None, None, None, None] / max(N_DP - 1, 1)
    row_pos = jnp.arange(SLAB, dtype=jnp.float32)[None, :, None, None, None] / (SLAB - 1)
    row_scale = jnp.sqrt((1.0 + 2.0 * slab_pos) * (1.0 + 2.0 * row_pos))
    drawn = jnp.clip(jax.random.normal(jax.random.fold_in(key, 7), shape, jnp.float32), -3.0, 3.0)
    offsets = block_offsets(key).reshape(N_DP, SLAB, HK, 1, HD)
    scales = head_scales(key).reshape(1, 1, HK, group, 1)
    full = (drawn + 0.8 * offsets) * scales * row_scale
    return full.reshape(N_DP, SLAB, HQ * HD).astype(jnp.bfloat16)


def set_ends(values, stream_key, least, largest):
    longest = values.shape.index(max(values.shape))
    spots = []
    for shift in (0, 1):
        where = [jax.random.randint(jax.random.fold_in(stream_key, axis), (), 0, length) for axis, length in enumerate(values.shape)]
        where[longest] = (where[longest] + shift) % values.shape[longest]
        spots.append(tuple(where))
    return values.at[spots[0]].set(least).at[spots[1]].set(largest)


def profile(amount, total, most, skew):
    weights = [(1 << 20) // math.isqrt(grade ** skew) + 1 for grade in range(2, amount + 1)]
    rest, given = total - most - (amount - 1), [1] * (amount - 1)
    while rest > 0:
        movable = [i for i in range(amount - 1) if given[i] < most]
        pool, left = sum([weights[i] for i in movable]), rest
        for i in movable:
            extra = min(most - given[i], max(1, left * weights[i] // pool), rest)
            given[i] = given[i] + extra
            rest = rest - extra
    return np.array([most] + given)


def ragged(stream_key, amount, total, limit, slope):
    if amount == 2:
        one = jax.random.randint(stream_key, (), max(1, total - limit), min(limit, total - 1) + 1)
        return jnp.stack([one, total - one])
    lengths = jnp.asarray(profile(amount, total, limit, slope), jnp.int32)
    couples = (amount - 1) // 2
    giver, taker = lengths[1:1 + 2 * couples:2], lengths[2:2 + 2 * couples:2]
    slack = jnp.minimum(giver - 1, limit - taker)
    shifted = jax.random.randint(jax.random.fold_in(stream_key, 1), (couples,), 0, 1 << 20) % (slack + 1)
    lengths = lengths.at[1:1 + 2 * couples:2].set(giver - shifted).at[2:2 + 2 * couples:2].set(taker + shifted)
    return lengths[jax.random.permutation(jax.random.fold_in(stream_key, 2), amount)]


def setup_inputs(seed: int = 0) -> dict:
    arg_keys = jax.random.split(jax.random.key(seed), 8)
    queries = draw_queries(jax.random.fold_in(arg_keys[7], 71), 0)
    key_states = draw_key_states(jax.random.fold_in(arg_keys[7], 71), 0)
    value_states = draw_value_states(jax.random.fold_in(arg_keys[7], 71), 0)
    targets = draw_targets(jax.random.fold_in(arg_keys[7], 71), 0)
    doc_blocks = jax.vmap(lambda own: ragged(own, DOCS, SLAB // BLOCK, MOST, 2))(jax.random.split(arg_keys[4], N_DP)).reshape((N_DP, DOCS)).astype(jnp.int32)
    doc_domain = set_ends(jax.random.randint(arg_keys[5], (N_DP, DOCS), 0, DOMAINS), jax.random.fold_in(arg_keys[5], 1), 0, DOMAINS - 1).astype(jnp.int32)
    domain_weight = jnp.clip(jnp.exp(jax.random.uniform(arg_keys[6], (DOMAINS,), jnp.float32, math.log(0.25), math.log(4.0))), 0.25, 4.0)
    return {"queries": queries, "key_states": key_states, "value_states": value_states, "targets": targets, "doc_blocks": doc_blocks, "doc_domain": doc_domain, "domain_weight": domain_weight}


def doc_index(positions, blocks_row):
    ends = jnp.cumsum(blocks_row) * BLOCK
    found = jnp.sum((positions[:, None] >= ends[None, :]).astype(jnp.int32), axis=1)
    return jnp.where(positions < 0, -1, found).astype(jnp.int32)


def token_domain(docs, domain_row):
    doc_count = domain_row.shape[0]
    picked = jnp.where(docs[:, None] == jnp.arange(doc_count, dtype=jnp.int32)[None, :], domain_row[None, :], 0)
    return jnp.sum(picked, axis=1).astype(jnp.int32)


def token_weight(domains, domain_weight):
    belongs = domains[:, None] == jnp.arange(DOMAINS, dtype=jnp.int32)[None, :]
    return jnp.sum(jnp.where(belongs, domain_weight[None, :], 0.0), axis=1)


def attend(query_blk, key_win, value_win, target_blk, row_weight, query_pos, key_pos, query_doc, key_doc):
    scaling = HD ** -0.5
    f32 = jnp.float32
    scores = jnp.einsum("qhgd,whd->hgqw", query_blk.astype(f32), key_win.astype(f32)) * scaling
    visible = (query_doc[:, None] == key_doc[None, :]) & (key_pos[None, :] <= query_pos[:, None]) & (key_doc[None, :] >= 0)
    scores = jnp.where(visible, scores, -1e30)
    row_max = jnp.max(scores, axis=-1, keepdims=True)
    raised = jnp.where(visible, jnp.exp(scores - row_max), 0.0)
    weights = raised / jnp.sum(raised, axis=-1, keepdims=True)
    weights_low = weights.astype(jnp.bfloat16)
    attn_out = jnp.einsum("hgqw,whd->qhgd", weights_low.astype(f32), value_win.astype(f32))
    error_term = attn_out - target_blk.astype(f32)
    token_loss = 0.5 * jnp.sum(error_term * error_term, axis=(1, 2, 3))
    grad_out = (row_weight[:, None, None, None] * error_term).astype(jnp.bfloat16)
    grad_value = jnp.einsum("hgqw,qhgd->whd", weights_low.astype(f32), grad_out.astype(f32))
    grad_weights = jnp.einsum("qhgd,whd->hgqw", grad_out.astype(f32), value_win.astype(f32))
    center = jnp.einsum("qhgd,qhgd->hgq", grad_out.astype(f32), attn_out)
    grad_scores = (weights * (grad_weights - center[..., None])).astype(jnp.bfloat16)
    grad_query = jnp.einsum("hgqw,whd->qhgd", grad_scores.astype(f32), key_win.astype(f32)) * scaling
    grad_key = jnp.einsum("hgqw,qhgd->whd", grad_scores.astype(f32), query_blk.astype(f32)) * scaling
    return token_loss, grad_query, grad_key, grad_value


def reference(queries, key_states, value_states, targets, doc_blocks, doc_domain, domain_weight):
    group = HQ // HK
    pad_rows = (MOST - 1) * BLOCK
    window_rows = pad_rows + BLOCK

    def one_slab(operands):
        query_slab, key_slab, value_slab, target_slab, blocks_row, domain_row = operands
        query_four = query_slab.reshape(SLAB, HK, group, HD)
        target_four = target_slab.reshape(SLAB, HK, group, HD)
        key_pad = jnp.concatenate([jnp.zeros((pad_rows, HK, HD), jnp.bfloat16), key_slab.reshape(SLAB, HK, HD)], axis=0)
        value_pad = jnp.concatenate([jnp.zeros((pad_rows, HK, HD), jnp.bfloat16), value_slab.reshape(SLAB, HK, HD)], axis=0)
        positions = jnp.arange(SLAB, dtype=jnp.int32)
        slab_docs = doc_index(positions, blocks_row)
        slab_domains = token_domain(slab_docs, domain_row)
        slab_weight = token_weight(slab_domains, domain_weight)
        pad_pos = jnp.arange(-pad_rows, SLAB, dtype=jnp.int32)
        pad_docs = doc_index(pad_pos, blocks_row)

        def block_step(running, block_id):
            key_acc, value_acc = running
            first_row = block_id * BLOCK
            first_pad = block_id * BLOCK
            token_loss, grad_query, grad_key, grad_value = attend(
                lax.dynamic_slice_in_dim(query_four, first_row, BLOCK, 0),
                lax.dynamic_slice_in_dim(key_pad, first_pad, window_rows, 0),
                lax.dynamic_slice_in_dim(value_pad, first_pad, window_rows, 0),
                lax.dynamic_slice_in_dim(target_four, first_row, BLOCK, 0),
                lax.dynamic_slice_in_dim(slab_weight, first_row, BLOCK, 0),
                lax.dynamic_slice_in_dim(positions, first_row, BLOCK, 0),
                lax.dynamic_slice_in_dim(pad_pos, first_pad, window_rows, 0),
                lax.dynamic_slice_in_dim(slab_docs, first_row, BLOCK, 0),
                lax.dynamic_slice_in_dim(pad_docs, first_pad, window_rows, 0))
            key_acc = lax.dynamic_update_slice_in_dim(key_acc, lax.dynamic_slice_in_dim(key_acc, first_pad, window_rows, 0) + grad_key, first_pad, 0)
            value_acc = lax.dynamic_update_slice_in_dim(value_acc, lax.dynamic_slice_in_dim(value_acc, first_pad, window_rows, 0) + grad_value, first_pad, 0)
            return (key_acc, value_acc), (token_loss, grad_query)

        zero_acc = jnp.zeros((pad_rows + SLAB, HK, HD), jnp.float32)
        (key_acc, value_acc), (block_loss, block_query) = lax.scan(block_step, (zero_acc, zero_acc), jnp.arange(SLAB // BLOCK, dtype=jnp.int32))
        grad_q = block_query.reshape(SLAB, HQ * HD).astype(jnp.bfloat16)
        grad_k = key_acc[pad_rows:].reshape(SLAB, HK * HD).astype(jnp.bfloat16)
        grad_v = value_acc[pad_rows:].reshape(SLAB, HK * HD).astype(jnp.bfloat16)
        slab_loss = block_loss.reshape(SLAB)
        belongs = slab_domains[:, None] == jnp.arange(DOMAINS, dtype=jnp.int32)[None, :]
        loss_sums = jnp.sum(jnp.where(belongs, slab_loss[:, None], 0.0), axis=0)
        row_counts = jnp.sum(belongs.astype(jnp.float32), axis=0)
        return grad_q, grad_k, grad_v, loss_sums, row_counts

    grad_q, grad_k, grad_v, loss_sums, row_counts = lax.map(one_slab, (queries, key_states, value_states, targets, doc_blocks, doc_domain))
    totals = jnp.sum(loss_sums, axis=0)
    tallies = jnp.sum(row_counts, axis=0)
    domain_loss = totals / (jnp.maximum(tallies, 1.0) * (HQ * HD))
    return grad_q, grad_k, grad_v, domain_loss
```

```python
import functools

import jax
import jax.numpy as jnp
from jax import lax
from jax.experimental import pallas as pl
from jax.experimental.pallas import tpu as pltpu
from jax.sharding import PartitionSpec as P

HD = 128
BLOCK = 128
MOST = 6
DOMAINS = 22
SCALE = HD**-0.5
LOG2E = 1.4426950408889634
HIDDEN = -1e30
HALO = (MOST - 1) * BLOCK
WINDOW = MOST * BLOCK
NT = (((1,), (1,)), ((), ()))
NN = (((1,), (0,)), ((), ()))
MESH = pl.DeviceIdType.MESH
f32 = jnp.float32
bf16 = jnp.bfloat16


def dot(a, b, dims):
    return lax.dot_general(a, b, dims, preferred_element_type=f32)


def kernel(
    n_ctx, n_dp, groups, per_group,
    blocks_ref, domain_ref, weight_ref, q_hbm, k_hbm, v_hbm, t_hbm,
    gq_hbm, gk_hbm, gv_hbm, loss_ref,
    qv, tv, gqv, kv, kT, vT, acc, own, sbuf, rbuf, outv, lossv, lsend, lrecv, tri,
    kv_sem, q_sem, t_sem, halo_send, halo_recv, grad_send, grad_recv, gq_sem, out_sem, l_send, l_recv,
):
    me = lax.axis_index("ctx")
    my_dp = lax.axis_index("dp")
    rows = 2 * BLOCK
    heads_w = per_group * HD

    def kv_copy(g, which):
        src = (k_hbm, v_hbm)[which]
        return pltpu.make_async_copy(
            src.at[:, pl.ds(pl.multiple_of(g * HD, HD), HD)],
            kv.at[g, which, pl.ds(HALO, rows), :],
            kv_sem.at[g, which],
        )

    def wide(ref, g):
        return ref.at[:, pl.ds(pl.multiple_of(g * heads_w, heads_w), heads_w)]

    def q_copy(g):
        return pltpu.make_async_copy(wide(q_hbm, g), wide(qv, g), q_sem.at[g])

    def t_copy(g):
        return pltpu.make_async_copy(wide(t_hbm, g), wide(tv, g), t_sem.at[g])

    def gq_copy(g):
        return pltpu.make_async_copy(wide(gqv, g), wide(gq_hbm, g), gq_sem.at[g])

    spans = ((1, HALO, HALO - rows, rows), (2, HALO, HALO - 2 * rows, rows), (3, HALO + BLOCK, 0, BLOCK))

    def halo_copy(g, i):
        ahead, first, there, count = spans[i]
        return pltpu.make_async_remote_copy(
            src_ref=kv.at[g, :, pl.ds(first, count), :],
            dst_ref=kv.at[g, :, pl.ds(there, count), :],
            send_sem=halo_send.at[g, i],
            recv_sem=halo_recv.at[g, i],
            device_id={"ctx": lax.rem(me + ahead, n_ctx)},
            device_id_type=MESH,
        )

    def grad_copy(g, i):
        ahead, _, there, count = spans[i]
        return pltpu.make_async_remote_copy(
            src_ref=sbuf.at[g, :, pl.ds(there, count), :],
            dst_ref=rbuf.at[g, :, pl.ds(there, count), :],
            send_sem=grad_send.at[g, i],
            recv_sem=grad_recv.at[g, i],
            device_id={"ctx": lax.rem(me + n_ctx - ahead, n_ctx)},
            device_id_type=MESH,
        )

    def out_copy(which):
        dst = (gk_hbm, gv_hbm)[which]
        return pltpu.make_async_copy(outv.at[which], dst, out_sem.at[which])

    def loss_copy(phase, i):
        if phase == 0:
            slot, target = me, {"ctx": lax.rem(me + i, n_ctx)}
        else:
            slot, target = my_dp, {"dp": lax.rem(my_dp + i, n_dp)}
        return pltpu.make_async_remote_copy(
            src_ref=lsend.at[phase],
            dst_ref=lrecv.at[phase, slot],
            send_sem=l_send.at[phase, i],
            recv_sem=l_recv.at[phase, i],
            device_id=target,
            device_id_type=MESH,
        )

    for g in range(groups):
        kv_copy(g, 0).start()
        kv_copy(g, 1).start()
    for g in range(groups):
        q_copy(g).start()
        t_copy(g).start()

    barrier = pltpu.get_barrier_semaphore()
    for i in range(1, n_ctx):
        pl.semaphore_signal(barrier, inc=1, device_id={"ctx": lax.rem(me + i, n_ctx)}, device_id_type=MESH)
    for i in range(1, n_dp):
        pl.semaphore_signal(barrier, inc=1, device_id={"dp": lax.rem(my_dp + i, n_dp)}, device_id_type=MESH)

    first_block = [2 * me, 2 * me + 1]
    doc_count = blocks_ref.shape[1]
    starts, omegas, domains = [], [], []
    for b in range(2):
        end = jnp.int32(0)
        start = jnp.int32(0)
        doc = jnp.int32(0)
        for i in range(doc_count - 1):
            end = end + blocks_ref[0, i]
            passed = first_block[b] >= end
            start = jnp.where(passed, end, start)
            doc = doc + jnp.where(passed, 1, 0)
        domain = domain_ref[0, doc]
        starts.append(start)
        domains.append(domain)
        omegas.append(weight_ref[domain])
    bias = [
        [jnp.where(first_block[b] - (MOST - 1) + j >= starts[b], 0.0, HIDDEN).astype(f32) for j in range(MOST - 1)]
        for b in range(2)
    ]
    key_row = lax.broadcasted_iota(jnp.int32, (BLOCK, heads_w), 0)
    query_col = lax.rem(lax.broadcasted_iota(jnp.int32, (BLOCK, heads_w), 1), BLOCK)
    tri[...] = jnp.where(key_row <= query_col, 0.0, HIDDEN).astype(f32)
    lossv[...] = jnp.zeros_like(lossv)

    pl.semaphore_wait(barrier, n_ctx - 1 + n_dp - 1)

    for g in range(groups):
        kv_copy(g, 0).wait()
        kv_copy(g, 1).wait()
        for i in range(3):
            halo_copy(g, i).start()

    def finish(g):
        for i in range(3):
            grad_copy(g, i).wait_recv()
        lanes = pl.ds(pl.multiple_of(g * HD, HD), HD)
        near = slice(HALO - rows, HALO)
        middle = slice(HALO - 2 * rows, HALO - rows)
        for which in range(2):
            total = own[g, which] + rbuf[g, which, near, :].astype(f32) + rbuf[g, which, middle, :].astype(f32)
            far = rbuf[g, which, 0:BLOCK, :].astype(f32)
            outv[which, 0:BLOCK, lanes] = total[0:BLOCK].astype(bf16)
            outv[which, BLOCK:rows, lanes] = (total[BLOCK:rows] + far).astype(bf16)

    def attend(g, b):
        first = BLOCK * b
        base = g * heads_w

        def columns(h):
            return pl.ds(pl.multiple_of(base + h * HD, HD), HD)

        key_win = kv[g, 0, first : first + WINDOW, :]
        value_win = kv[g, 1, first : first + WINDOW, :]
        query = jnp.concatenate([qv[first : first + BLOCK, columns(h)] for h in range(per_group)], 0)
        target = jnp.concatenate([tv[first : first + BLOCK, columns(h)].astype(f32).T for h in range(per_group)], 1)
        scores = dot(key_win, query, NT)
        parts, top = [], None
        for j in range(MOST):
            part = scores[BLOCK * j : BLOCK * (j + 1)]
            if j == MOST - 1:
                part = part + tri[...]
            parts.append(part)
            part_top = jnp.max(part.reshape(BLOCK // 8, 8, heads_w), axis=0)
            if j < MOST - 1:
                part_top = part_top + bias[b][j]
            top = part_top if top is None else jnp.maximum(top, part_top)
        shift = jnp.max(top, axis=0, keepdims=True) * (SCALE * LOG2E)
        raised, sums = [], None
        for j in range(MOST):
            off = shift if j == MOST - 1 else shift - bias[b][j]
            part = jnp.exp2(parts[j] * (SCALE * LOG2E) - off)
            raised.append(part)
            part_sum = jnp.sum(part.reshape(BLOCK // 8, 8, heads_w), axis=0)
            sums = part_sum if sums is None else sums + part_sum
        inverse = 1.0 / jnp.sum(sums, axis=0, keepdims=True)
        raised = jnp.concatenate(raised, 0)
        raised_low = raised.astype(bf16)
        out = dot(vT[:, first : first + WINDOW], raised_low, NN) * inverse
        error = out - target
        squares = error * error
        lossv[b] += jnp.sum(squares.reshape(HD // 8, 8, heads_w), axis=0)
        grad_out = (error * (inverse * omegas[b])).astype(bf16)
        center = jnp.sum(grad_out.astype(f32) * out, axis=0, keepdims=True)
        grad_probs = dot(value_win, grad_out, NN)
        grad_scores = (raised * (grad_probs - center)).astype(bf16)
        grad_query = dot(kT[:, first : first + WINDOW], grad_scores, NN) * SCALE
        for h in range(per_group):
            gqv[first : first + BLOCK, columns(h)] = grad_query[:, HD * h : HD * (h + 1)].T.astype(bf16)
        grad_value = dot(raised_low, grad_out, NT)
        grad_key = dot(grad_scores, query, NN) * SCALE
        for which, part in ((0, grad_key), (1, grad_value)):
            if b == 0:
                acc[which, 0:WINDOW, :] = part
            else:
                acc[which, BLOCK:WINDOW, :] += part[0 : WINDOW - BLOCK]
                acc[which, WINDOW:, :] = part[WINDOW - BLOCK :]

    def step(g, carry):
        for i in range(3):
            halo_copy(g, i).wait_recv()
        q_copy(g).wait()
        t_copy(g).wait()
        kT[...] = kv[g, 0].T
        vT[...] = kv[g, 1].T
        attend(g, 0)
        attend(g, 1)
        for which in range(2):
            sbuf[g, which] = acc[which, 0:HALO, :].astype(bf16)
            own[g, which] = acc[which, HALO:, :]
        for i in (2, 1, 0):
            grad_copy(g, i).start()
        gq_copy(g).start()

        @pl.when(g > 0)
        def _():
            finish(g - 1)

        return carry

    lax.fori_loop(0, groups, step, 0)

    lane = lax.broadcasted_iota(jnp.int32, (8, HD), 1)
    line = lax.broadcasted_iota(jnp.int32, (8, HD), 0)
    tile = jnp.zeros((8, HD), f32)
    for b in range(2):
        block_loss = 0.5 * jnp.sum(jnp.sum(lossv[b], axis=0, keepdims=True), axis=1, keepdims=True)
        picked = jnp.where(line == 0, block_loss, jnp.where(line == 1, float(BLOCK), 0.0))
        tile = tile + jnp.where(lane == domains[b], picked, 0.0)
    for phase in range(2):
        n = (n_ctx, n_dp)[phase]
        lsend[phase] = tile
        lrecv[phase, (me, my_dp)[phase]] = tile
        for i in range(1, n):
            loss_copy(phase, i).start()
        if phase == 0:
            finish(groups - 1)
            out_copy(0).start()
            out_copy(1).start()
        for i in range(1, n):
            loss_copy(phase, i).wait()
        tile = lrecv[phase, 0]
        for i in range(1, n):
            tile = tile + lrecv[phase, i]
    loss_ref[...] = tile[0:1] / (jnp.maximum(tile[1:2], 1.0) * float(groups * per_group * HD))

    for g in range(groups):
        for i in range(3):
            halo_copy(g, i).wait_send()
            grad_copy(g, i).wait_send()
        gq_copy(g).wait()
    out_copy(0).wait()
    out_copy(1).wait()


def on_device(n_ctx, n_dp, queries, key_states, value_states, targets, doc_blocks, doc_domain, domain_weight):
    rows, q_width = queries.shape[1:]
    kv_width = key_states.shape[2]
    groups = kv_width // HD
    per_group = q_width // kv_width
    heads_w = per_group * HD
    any_space = pl.BlockSpec(memory_space=pl.ANY)
    smem = pl.BlockSpec(memory_space=pltpu.SMEM)
    dma = pltpu.SemaphoreType.DMA
    span = HALO + rows
    most_peers = max(n_ctx, n_dp)
    gq, gk, gv, loss = pl.pallas_call(
        functools.partial(kernel, n_ctx, n_dp, groups, per_group),
        out_shape=(
            jax.ShapeDtypeStruct((rows, q_width), bf16),
            jax.ShapeDtypeStruct((rows, kv_width), bf16),
            jax.ShapeDtypeStruct((rows, kv_width), bf16),
            jax.ShapeDtypeStruct((1, HD), f32),
        ),
        in_specs=[smem, smem, smem, any_space, any_space, any_space, any_space],
        out_specs=(any_space, any_space, any_space, pl.BlockSpec(memory_space=pltpu.VMEM)),
        scratch_shapes=[
            pltpu.VMEM((rows, q_width), bf16),
            pltpu.VMEM((rows, q_width), bf16),
            pltpu.VMEM((rows, q_width), bf16),
            pltpu.VMEM((groups, 2, span, HD), bf16),
            pltpu.VMEM((HD, span), bf16),
            pltpu.VMEM((HD, span), bf16),
            pltpu.VMEM((2, span, HD), f32),
            pltpu.VMEM((groups, 2, rows, HD), f32),
            pltpu.VMEM((groups, 2, HALO, HD), bf16),
            pltpu.VMEM((groups, 2, HALO, HD), bf16),
            pltpu.VMEM((2, rows, kv_width), bf16),
            pltpu.VMEM((2, 8, heads_w), f32),
            pltpu.VMEM((2, 8, HD), f32),
            pltpu.VMEM((2, most_peers, 8, HD), f32),
            pltpu.VMEM((BLOCK, heads_w), f32),
            dma((groups, 2)),
            dma((groups,)),
            dma((groups,)),
            dma((groups, 3)),
            dma((groups, 3)),
            dma((groups, 3)),
            dma((groups, 3)),
            dma((groups,)),
            dma((2,)),
            dma((2, most_peers)),
            dma((2, most_peers)),
        ],
        compiler_params=pltpu.CompilerParams(collective_id=0, has_side_effects=True, vmem_limit_bytes=60 << 20),
    )(doc_blocks, doc_domain, domain_weight, queries[0], key_states[0], value_states[0], targets[0])
    return gq[None], gk[None], gv[None], loss[0, :DOMAINS]


def solution(mesh):
    placed = (
        P("dp", "ctx", None),
        P("dp", "ctx", None),
        P("dp", "ctx", None),
        P("dp", "ctx", None),
        P("dp", None),
        P("dp", None),
        P(),
    )
    return jax.shard_map(
        functools.partial(on_device, mesh.shape["ctx"], mesh.shape["dp"]),
        mesh=mesh,
        in_specs=placed,
        out_specs=(P("dp", "ctx", None), P("dp", "ctx", None), P("dp", "ctx", None), P()),
        check_vma=False,
    )
```

```python
import functools

import jax
import jax.numpy as jnp
from jax import lax
from jax.experimental import pallas as pl
from jax.experimental.pallas import tpu as pltpu
from jax.sharding import PartitionSpec as P

HD = 128
BLOCK = 128
MOST = 6
DOMAINS = 22
SCALE = HD**-0.5
LOG2E = 1.4426950408889634
HIDDEN = -1e30
HALO = (MOST - 1) * BLOCK
WINDOW = MOST * BLOCK
NT = (((1,), (1,)), ((), ()))
NN = (((1,), (0,)), ((), ()))
MESH = pl.DeviceIdType.MESH
f32 = jnp.float32
bf16 = jnp.bfloat16


def dot(a, b, dims):
    return lax.dot_general(a, b, dims, preferred_element_type=f32)


def kernel(
    n_ctx, n_dp, groups, per_group,
    blocks_ref, domain_ref, weight_ref, q_hbm, k_hbm, v_hbm, t_hbm,
    gq_ref, gk_ref, gv_ref, loss_ref,
    qv, tv, tT, kv, kT, vT, raised, gout, center, acc, own, keep, sbuf, rbuf, lossv, lsend, lrecv, tri,
    kv_sem, q_sem, t_sem, halo_send, halo_recv, grad_send, grad_recv, l_send, l_recv,
):
    me = lax.axis_index("ctx")
    my_dp = lax.axis_index("dp")
    rows = 2 * BLOCK
    heads_w = per_group * HD

    def kv_copy(g, which):
        src = (k_hbm, v_hbm)[which]
        return pltpu.make_async_copy(
            src.at[:, pl.ds(pl.multiple_of(g * HD, HD), HD)],
            kv.at[g, which, pl.ds(HALO, rows), :],
            kv_sem.at[g, which],
        )

    def wide(ref, g):
        return ref.at[:, pl.ds(pl.multiple_of(g * heads_w, heads_w), heads_w)]

    def q_copy(g):
        return pltpu.make_async_copy(wide(q_hbm, g), wide(qv, g), q_sem.at[g])

    def t_copy(g):
        return pltpu.make_async_copy(wide(t_hbm, g), wide(tv, g), t_sem.at[g])

    halos = ((1, HALO, HALO - rows, rows), (3, HALO + BLOCK, 0, BLOCK), (1, HALO - rows, BLOCK, BLOCK), (-1, 0, 2 * BLOCK, BLOCK), (2, HALO, BLOCK, rows))

    def halo_copy(g, i):
        ahead, first, there, count = halos[i]
        return pltpu.make_async_remote_copy(
            src_ref=kv.at[g, :, pl.ds(first, count), :],
            dst_ref=kv.at[g, :, pl.ds(there, count), :],
            send_sem=halo_send.at[g, i],
            recv_sem=halo_recv.at[g, i],
            device_id={"ctx": lax.rem(me + (n_ctx + ahead), n_ctx)},
            device_id_type=MESH,
        )


    def grad_copy(g, i):
        steps = (-1, 1, -1, -1, -3)[i]
        return pltpu.make_async_remote_copy(
            src_ref=sbuf.at[g, i],
            dst_ref=rbuf.at[g, i],
            send_sem=grad_send.at[g, i],
            recv_sem=grad_recv.at[g, i],
            device_id={"ctx": lax.rem(me + (n_ctx + steps), n_ctx)},
            device_id_type=MESH,
        )

    def loss_copy(phase, i):
        if phase == 0:
            slot, target = me, {"ctx": lax.rem(me + i, n_ctx)}
        else:
            slot, target = my_dp, {"dp": lax.rem(my_dp + i, n_dp)}
        return pltpu.make_async_remote_copy(
            src_ref=lsend.at[phase],
            dst_ref=lrecv.at[phase, slot],
            send_sem=l_send.at[phase, i],
            recv_sem=l_recv.at[phase, i],
            device_id=target,
            device_id_type=MESH,
        )

    barrier = pltpu.get_barrier_semaphore()
    for i in range(1, n_ctx):
        pl.semaphore_signal(barrier, inc=1, device_id={"ctx": lax.rem(me + i, n_ctx)}, device_id_type=MESH)
    for i in range(1, n_dp):
        pl.semaphore_signal(barrier, inc=1, device_id={"dp": lax.rem(my_dp + i, n_dp)}, device_id_type=MESH)
    for g in range(groups):
        kv_copy(g, 0).start()
        kv_copy(g, 1).start()
    for g in range(groups):
        q_copy(g).start()
        t_copy(g).start()

    first_block = [2 * me, 2 * me + 1]
    doc_count = blocks_ref.shape[1]
    starts, omegas, domains = [], [], []
    for b in range(2):
        end = jnp.int32(0)
        start = jnp.int32(0)
        doc = jnp.int32(0)
        for i in range(doc_count - 1):
            end = end + blocks_ref[0, i]
            passed = first_block[b] >= end
            start = jnp.where(passed, end, start)
            doc = doc + jnp.where(passed, 1, 0)
        domain = domain_ref[0, doc]
        starts.append(start)
        domains.append(domain)
        omegas.append(weight_ref[domain])
    bias = [
        [jnp.where(first_block[b] - (MOST - 1) + j >= starts[b], 0.0, HIDDEN).astype(f32) for j in range(MOST - 1)]
        for b in range(2)
    ]
    key_row = lax.broadcasted_iota(jnp.int32, (BLOCK, heads_w), 0)
    query_col = lax.rem(lax.broadcasted_iota(jnp.int32, (BLOCK, heads_w), 1), BLOCK)
    tri[...] = jnp.where(key_row <= query_col, 0.0, HIDDEN).astype(f32)
    lossv[...] = jnp.zeros_like(lossv)

    def send_halo(g):
        kv_copy(g, 0).wait()
        kv_copy(g, 1).wait()
        halo_copy(g, 0).start()
        halo_copy(g, 1).start()

    def relay_halo(g):
        halo_copy(g, 0).wait_recv()
        halo_copy(g, 1).wait_recv()
        halo_copy(g, 2).start()
        halo_copy(g, 3).start()

    def send_grads(g):
        for which in range(2):
            sbuf[g, 0, which] = acc[which, BLOCK : 2 * BLOCK, :].astype(bf16)
            sbuf[g, 1, which] = acc[which, 2 * BLOCK : 3 * BLOCK, :].astype(bf16)
            sbuf[g, 2, which] = acc[which, 4 * BLOCK : HALO, :].astype(bf16)
        for i in range(3):
            grad_copy(g, i).start()

        for which in range(2):
            keep[g % 2, 0, which] = acc[which, 3 * BLOCK : 4 * BLOCK, :]
            keep[g % 2, 1, which] = acc[which, 0:BLOCK, :]

        for which in range(2):
            own[g, which] = acc[which, HALO:, :]

    def relay_grads(g):
        for i in range(2):
            grad_copy(g, i).wait_recv()
            for which in range(2):
                sbuf[g, 3 + i, which] = (keep[g % 2, i, which] + rbuf[g, i, which].astype(f32)).astype(bf16)
            grad_copy(g, 3 + i).start()

    def finish(g):
        for i in range(2, 5):
            grad_copy(g, i).wait_recv()
        lanes = pl.ds(pl.multiple_of(g * HD, HD), HD)
        for which, out_ref in ((0, gk_ref), (1, gv_ref)):
            total = own[g, which, 0:BLOCK, :] + rbuf[g, 3, which].astype(f32)
            out_ref[0:BLOCK, lanes] = total.astype(bf16)
            total = own[g, which, BLOCK:rows, :] + rbuf[g, 2, which].astype(f32) + rbuf[g, 4, which].astype(f32)
            out_ref[BLOCK:rows, lanes] = total.astype(bf16)

    lane = lax.broadcasted_iota(jnp.int32, (8, HD), 1)
    line = lax.broadcasted_iota(jnp.int32, (8, HD), 0)

    def start_losses(phase, tile):
        lsend[phase] = tile
        lrecv[phase, (me, my_dp)[phase]] = tile
        for i in range(1, (n_ctx, n_dp)[phase]):
            loss_copy(phase, i).start()

    def add_losses(phase):
        n = (n_ctx, n_dp)[phase]
        for i in range(1, n):
            loss_copy(phase, i).wait()
        tile = lrecv[phase, 0]
        for i in range(1, n):
            tile = tile + lrecv[phase, i]
        return tile

    def slab_losses():
        tile = jnp.zeros((8, HD), f32)
        for b in range(2):
            block_loss = 0.5 * jnp.sum(jnp.sum(lossv[b], axis=0, keepdims=True), axis=1, keepdims=True)
            picked = jnp.where(line == 0, block_loss, jnp.where(line == 1, float(BLOCK), 0.0))
            tile = tile + jnp.where(lane == domains[b], picked, 0.0)
        start_losses(0, tile)

    def turn_targets():
        def turn(g, carry):
            t_copy(g).wait()
            for b in range(2):
                for h in range(per_group):
                    columns = pl.ds(pl.multiple_of(g * heads_w + h * HD, HD), HD)
                    tT[g, b, :, HD * h : HD * (h + 1)] = tv[BLOCK * b : BLOCK * (b + 1), columns].T
            return carry

        lax.fori_loop(0, groups, turn, 0)

    def columns(g, h):
        return pl.ds(pl.multiple_of(g * heads_w + h * HD, HD), HD)

    def queries_of(g, b):
        first = BLOCK * b
        return jnp.concatenate([qv[first : first + BLOCK, columns(g, h)] for h in range(per_group)], 0)

    def forward(g, slot):
        @pl.when(g == 0)
        def _():
            for i in (0, 1, 4):
                halo_copy(0, i).wait_recv()

        @pl.when(g > 0)
        def _():
            halo_copy(g, 2).wait_recv()
            halo_copy(g, 3).wait_recv()

        q_copy(g).wait()
        kT[slot] = kv[g, 0].T
        vT[...] = kv[g, 1].T
        for b in range(2):
            first = BLOCK * b
            scores = dot(kv[g, 0, first : first + WINDOW, :], queries_of(g, b), NT)
            parts, top = [], None
            for j in range(MOST):
                part = scores[BLOCK * j : BLOCK * (j + 1)]
                if j == MOST - 1:
                    part = part + tri[...]
                parts.append(part)
                part_top = jnp.max(part.reshape(BLOCK // 8, 8, heads_w), axis=0)
                if j < MOST - 1:
                    part_top = part_top + bias[b][j]
                top = part_top if top is None else jnp.maximum(top, part_top)
            shift = jnp.max(top, axis=0, keepdims=True) * (SCALE * LOG2E)
            raised_low, sums = [], None
            for j in range(MOST):
                off = shift if j == MOST - 1 else shift - bias[b][j]
                part = jnp.exp2(parts[j] * (SCALE * LOG2E) - off)
                raised_low.append(part.astype(bf16))
                part_sum = jnp.sum(part.reshape(BLOCK // 8, 8, heads_w), axis=0)
                sums = part_sum if sums is None else sums + part_sum
            inverse = 1.0 / jnp.sum(sums, axis=0, keepdims=True)
            raised_low = jnp.concatenate(raised_low, 0)
            raised[slot, b] = raised_low
            out = dot(vT[:, first : first + WINDOW], raised_low, NN) * inverse
            error = out - tT[g, b].astype(f32)
            squares = error * error
            lossv[b] += jnp.sum(squares.reshape(HD // 8, 8, heads_w), axis=0)
            grad_out = (error * (inverse * omegas[b])).astype(bf16)
            gout[slot, b] = grad_out
            center[slot, b] = jnp.sum(grad_out.astype(f32) * out, axis=0, keepdims=True)

    def backward(g, slot, between):
        grad_scores = []
        for b in range(2):
            first = BLOCK * b
            grad_out = gout[slot, b]
            grad_probs = dot(kv[g, 1, first : first + WINDOW, :], grad_out, NN)
            grad_score = (raised[slot, b].astype(f32) * (grad_probs - center[slot, b])).astype(bf16)
            grad_scores.append(grad_score)
            grad_value = dot(raised[slot, b], grad_out, NT)
            grad_key = dot(grad_score, queries_of(g, b), NN) * SCALE
            for which, part in ((0, grad_key), (1, grad_value)):
                if b == 0:
                    acc[which, 0:WINDOW, :] = part
                else:
                    acc[which, BLOCK:WINDOW, :] += part[0 : WINDOW - BLOCK]
                    acc[which, WINDOW:, :] = part[WINDOW - BLOCK :]
        between()
        send_grads(g)
        for b in range(2):
            first = BLOCK * b
            grad_query = dot(kT[slot, :, first : first + WINDOW], grad_scores[b], NN) * SCALE
            for h in range(per_group):
                gq_ref[first : first + BLOCK, columns(g, h)] = grad_query[:, HD * h : HD * (h + 1)].T.astype(bf16)

    def first_groups(g, carry):
        forward(g, 0)

        @pl.when(g == 0)
        def _():
            relay_halo(1)
            send_halo(2)
            send_halo(3)

        @pl.when(g == 1)
        def _():
            relay_halo(2)
            relay_halo(3)

        def between():
            @pl.when(g == 1)
            def _():
                relay_grads(0)

        backward(g, 0, between)
        return carry

    def last_forward(i, carry):
        forward(2 + i, i)
        return carry

    def last_backward(i, carry):
        def between():
            @pl.when(i == 0)
            def _():
                finish(0)

            @pl.when(i == 1)
            def _():
                start_losses(1, add_losses(0))

        backward(2 + i, i, between)
        return carry

    pl.semaphore_wait(barrier, n_ctx - 1 + n_dp - 1)
    send_halo(0)
    halo_copy(0, 4).start()
    send_halo(1)
    turn_targets()
    lax.fori_loop(0, 2, first_groups, 0)
    lax.fori_loop(0, 2, last_forward, 0)
    slab_losses()
    relay_grads(1)
    lax.fori_loop(0, 2, last_backward, 0)
    relay_grads(2)
    finish(1)
    relay_grads(3)
    finish(2)
    finish(3)
    tile = add_losses(1)
    loss_ref[...] = tile[0:1] / (jnp.maximum(tile[1:2], 1.0) * float(groups * per_group * HD))
    for g in range(groups):
        for i in (0, 1, 4) if g == 0 else (0, 1, 2, 3):
            halo_copy(g, i).wait_send()
        for i in range(5):
            grad_copy(g, i).wait_send()


def write(gq_ref, gk_ref, gv_ref, loss_ref, gq_hbm, gk_hbm, gv_hbm, loss_out, sems):
    pairs = ((gq_ref, gq_hbm), (gk_ref, gk_hbm), (gv_ref, gv_hbm))
    copies = [pltpu.make_async_copy(src, dst, sems.at[i]) for i, (src, dst) in enumerate(pairs)]
    for copy in copies:
        copy.start()
    loss_out[...] = loss_ref[0, 0:DOMAINS]
    for copy in copies:
        copy.wait()


def on_device(n_ctx, n_dp, queries, key_states, value_states, targets, doc_blocks, doc_domain, domain_weight):
    rows, q_width = queries.shape[1:]
    kv_width = key_states.shape[2]
    groups = kv_width // HD
    per_group = q_width // kv_width
    heads_w = per_group * HD
    any_space = pl.BlockSpec(memory_space=pl.ANY)
    smem = pl.BlockSpec(memory_space=pltpu.SMEM)
    vmem = pl.BlockSpec(memory_space=pltpu.VMEM)
    dma = pltpu.SemaphoreType.DMA
    span = HALO + rows
    most_peers = max(n_ctx, n_dp)
    gq, gk, gv, loss = pl.pallas_call(
        functools.partial(kernel, n_ctx, n_dp, groups, per_group),
        out_shape=(
            pltpu.VMEM((rows, q_width), bf16),
            pltpu.VMEM((rows, kv_width), bf16),
            pltpu.VMEM((rows, kv_width), bf16),
            pltpu.VMEM((1, HD), f32),
        ),
        in_specs=[smem, smem, smem, any_space, any_space, any_space, any_space],
        out_specs=(vmem,) * 4,
        scratch_shapes=[
            pltpu.VMEM((rows, q_width), bf16),
            pltpu.VMEM((rows, q_width), bf16),
            pltpu.VMEM((groups, 2, HD, heads_w), bf16),
            pltpu.VMEM((groups, 2, span, HD), bf16),
            pltpu.VMEM((2, HD, span), bf16),
            pltpu.VMEM((HD, span), bf16),
            pltpu.VMEM((2, 2, WINDOW, heads_w), bf16),
            pltpu.VMEM((2, 2, HD, heads_w), bf16),
            pltpu.VMEM((2, 2, 1, heads_w), f32),
            pltpu.VMEM((2, span, HD), f32),
            pltpu.VMEM((groups, 2, rows, HD), f32),
            pltpu.VMEM((2, 2, 2, BLOCK, HD), f32),
            pltpu.VMEM((groups, 5, 2, BLOCK, HD), bf16),
            pltpu.VMEM((groups, 5, 2, BLOCK, HD), bf16),
            pltpu.VMEM((2, 8, heads_w), f32),
            pltpu.VMEM((2, 8, HD), f32),
            pltpu.VMEM((2, most_peers, 8, HD), f32),
            pltpu.VMEM((BLOCK, heads_w), f32),
            dma((groups, 2)),
            dma((groups,)),
            dma((groups,)),
            dma((groups, 5)),
            dma((groups, 5)),
            dma((groups, 5)),
            dma((groups, 5)),
            dma((2, most_peers)),
            dma((2, most_peers)),
        ],
        compiler_params=pltpu.CompilerParams(collective_id=0, has_side_effects=True, vmem_limit_bytes=56 << 20),
    )(doc_blocks, doc_domain, domain_weight, queries[0], key_states[0], value_states[0], targets[0])
    gq, gk, gv, loss = pl.pallas_call(
        write,
        out_shape=(
            jax.ShapeDtypeStruct((rows, q_width), bf16),
            jax.ShapeDtypeStruct((rows, kv_width), bf16),
            jax.ShapeDtypeStruct((rows, kv_width), bf16),
            jax.ShapeDtypeStruct((DOMAINS,), f32),
        ),
        in_specs=[vmem] * 4,
        out_specs=(any_space, any_space, any_space, vmem),
        scratch_shapes=[dma((3,))],
    )(*(pltpu.with_memory_space_constraint(x, pltpu.VMEM) for x in (gq, gk, gv, loss)))
    return gq[None], gk[None], gv[None], loss


def solution(mesh):
    placed = (
        P("dp", "ctx", None),
        P("dp", "ctx", None),
        P("dp", "ctx", None),
        P("dp", "ctx", None),
        P("dp", None),
        P("dp", None),
        P(),
    )
    return jax.shard_map(
        functools.partial(on_device, mesh.shape["ctx"], mesh.shape["dp"]),
        mesh=mesh,
        in_specs=placed,
        out_specs=(P("dp", "ctx", None), P("dp", "ctx", None), P("dp", "ctx", None), P()),
        check_vma=False,
    )
```

```python
import functools

import jax
import jax.numpy as jnp
from jax import lax
from jax.experimental import pallas as pl
from jax.experimental.pallas import tpu as pltpu
from jax.sharding import PartitionSpec as P

HD = 128
BLOCK = 128
MOST = 6
DOMAINS = 22
SCALE = HD**-0.5
LOG2E = 1.4426950408889634
HIDDEN = -1e30
HALO = (MOST - 1) * BLOCK
WINDOW = MOST * BLOCK
NT = (((1,), (1,)), ((), ()))
NN = (((1,), (0,)), ((), ()))
MESH = pl.DeviceIdType.MESH
f32 = jnp.float32
bf16 = jnp.bfloat16


def dot(a, b, dims):
    return lax.dot_general(a, b, dims, preferred_element_type=f32)


def kernel(
    n_ctx, n_dp, groups, per_group,
    blocks_ref, domain_ref, weight_ref, q_hbm, k_hbm, v_hbm, t_hbm,
    gq_ref, gk_ref, gv_ref, loss_ref,
    qv, tv, tT, kv, kT, vT, raised, gout, center, acc, own, keep, sbuf, rbuf, lossv, lsend, lrecv, tri,
    kv_sem, q_sem, t_sem, halo_send, halo_recv, grad_send, grad_recv, l_send, l_recv,
):
    me = lax.axis_index("ctx")
    my_dp = lax.axis_index("dp")
    rows = 2 * BLOCK
    heads_w = per_group * HD

    def kv_copy(g, which):
        src = (k_hbm, v_hbm)[which]
        return pltpu.make_async_copy(
            src.at[:, pl.ds(pl.multiple_of(g * HD, HD), HD)],
            kv.at[g, which, pl.ds(HALO, rows), :],
            kv_sem.at[g, which],
        )

    def wide(ref, g):
        return ref.at[:, pl.ds(pl.multiple_of(g * heads_w, heads_w), heads_w)]

    def q_copy(g):
        return pltpu.make_async_copy(wide(q_hbm, g), wide(qv, g), q_sem.at[g])

    def t_copy(g):
        return pltpu.make_async_copy(wide(t_hbm, g), wide(tv, g), t_sem.at[g])

    halos = ((1, HALO, HALO - rows, rows), (3, HALO + BLOCK, 0, BLOCK), (1, HALO - rows, BLOCK, BLOCK), (-1, 0, 2 * BLOCK, BLOCK), (2, HALO, BLOCK, BLOCK))

    def halo_copy(g, i):
        ahead, first, there, count = halos[i]
        return pltpu.make_async_remote_copy(
            src_ref=kv.at[g, :, pl.ds(first, count), :],
            dst_ref=kv.at[g, :, pl.ds(there, count), :],
            send_sem=halo_send.at[g, i],
            recv_sem=halo_recv.at[g, i],
            device_id={"ctx": lax.rem(me + (n_ctx + ahead), n_ctx)},
            device_id_type=MESH,
        )


    def grad_copy(g, i):
        steps = (-1, 1, -1, -1, -3)[i]
        return pltpu.make_async_remote_copy(
            src_ref=sbuf.at[g, i],
            dst_ref=rbuf.at[g, i],
            send_sem=grad_send.at[g, i],
            recv_sem=grad_recv.at[g, i],
            device_id={"ctx": lax.rem(me + (n_ctx + steps), n_ctx)},
            device_id_type=MESH,
        )

    def loss_copy(phase, i):
        if phase == 0:
            slot, target = me, {"ctx": lax.rem(me + i, n_ctx)}
        else:
            slot, target = my_dp, {"dp": lax.rem(my_dp + i, n_dp)}
        return pltpu.make_async_remote_copy(
            src_ref=lsend.at[phase],
            dst_ref=lrecv.at[phase, slot],
            send_sem=l_send.at[phase, i],
            recv_sem=l_recv.at[phase, i],
            device_id=target,
            device_id_type=MESH,
        )

    barrier = pltpu.get_barrier_semaphore()
    for i in range(1, n_ctx):
        pl.semaphore_signal(barrier, inc=1, device_id={"ctx": lax.rem(me + i, n_ctx)}, device_id_type=MESH)
    for i in range(1, n_dp):
        pl.semaphore_signal(barrier, inc=1, device_id={"dp": lax.rem(my_dp + i, n_dp)}, device_id_type=MESH)
    for g in range(groups):
        kv_copy(g, 0).start()
        kv_copy(g, 1).start()
    for g in range(groups):
        q_copy(g).start()
        t_copy(g).start()

    first_block = [2 * me, 2 * me + 1]
    doc_count = blocks_ref.shape[1]
    starts, omegas, domains = [], [], []
    for b in range(2):
        end = jnp.int32(0)
        start = jnp.int32(0)
        doc = jnp.int32(0)
        for i in range(doc_count - 1):
            end = end + blocks_ref[0, i]
            passed = first_block[b] >= end
            start = jnp.where(passed, end, start)
            doc = doc + jnp.where(passed, 1, 0)
        domain = domain_ref[0, doc]
        starts.append(start)
        domains.append(domain)
        omegas.append(weight_ref[domain])
    bias = [
        [jnp.where(first_block[b] - (MOST - 1) + j >= starts[b], 0.0, HIDDEN).astype(f32) for j in range(MOST - 1)]
        for b in range(2)
    ]
    key_row = lax.broadcasted_iota(jnp.int32, (BLOCK, heads_w), 0)
    query_col = lax.rem(lax.broadcasted_iota(jnp.int32, (BLOCK, heads_w), 1), BLOCK)
    tri[...] = jnp.where(key_row <= query_col, 0.0, HIDDEN).astype(f32)
    lossv[...] = jnp.zeros_like(lossv)

    def send_halo(g):
        kv_copy(g, 0).wait()
        kv_copy(g, 1).wait()
        halo_copy(g, 0).start()
        halo_copy(g, 1).start()

    def relay_halo(g):
        halo_copy(g, 0).wait_recv()
        halo_copy(g, 1).wait_recv()
        halo_copy(g, 2).start()
        halo_copy(g, 3).start()

    def send_grads(g):
        for which in range(2):
            sbuf[g, 0, which] = acc[which, BLOCK : 2 * BLOCK, :].astype(bf16)
            sbuf[g, 1, which] = acc[which, 2 * BLOCK : 3 * BLOCK, :].astype(bf16)
            sbuf[g, 2, which] = acc[which, 4 * BLOCK : HALO, :].astype(bf16)
        for i in range(3):
            grad_copy(g, i).start()

        for which in range(2):
            keep[g % 2, 0, which] = acc[which, 3 * BLOCK : 4 * BLOCK, :]
            keep[g % 2, 1, which] = acc[which, 0:BLOCK, :]

        for which in range(2):
            own[g, which] = acc[which, HALO:, :]

    def relay_grads(g):
        for i in range(2):
            grad_copy(g, i).wait_recv()
            for which in range(2):
                sbuf[g, 3 + i, which] = (keep[g % 2, i, which] + rbuf[g, i, which].astype(f32)).astype(bf16)
            grad_copy(g, 3 + i).start()

    def finish(g):
        for i in range(2, 5):
            grad_copy(g, i).wait_recv()
        lanes = pl.ds(pl.multiple_of(g * HD, HD), HD)
        for which, out_ref in ((0, gk_ref), (1, gv_ref)):
            total = own[g, which, 0:BLOCK, :] + rbuf[g, 3, which].astype(f32)
            out_ref[0:BLOCK, lanes] = total.astype(bf16)
            total = own[g, which, BLOCK:rows, :] + rbuf[g, 2, which].astype(f32) + rbuf[g, 4, which].astype(f32)
            out_ref[BLOCK:rows, lanes] = total.astype(bf16)

    lane = lax.broadcasted_iota(jnp.int32, (8, HD), 1)
    line = lax.broadcasted_iota(jnp.int32, (8, HD), 0)

    def start_losses(phase, tile):
        lsend[phase] = tile
        lrecv[phase, (me, my_dp)[phase]] = tile
        for i in range(1, (n_ctx, n_dp)[phase]):
            loss_copy(phase, i).start()

    def add_losses(phase):
        n = (n_ctx, n_dp)[phase]
        for i in range(1, n):
            loss_copy(phase, i).wait()
        tile = lrecv[phase, 0]
        for i in range(1, n):
            tile = tile + lrecv[phase, i]
        return tile

    def slab_losses():
        tile = jnp.zeros((8, HD), f32)
        for b in range(2):
            block_loss = 0.5 * jnp.sum(jnp.sum(lossv[b], axis=0, keepdims=True), axis=1, keepdims=True)
            picked = jnp.where(line == 0, block_loss, jnp.where(line == 1, float(BLOCK), 0.0))
            tile = tile + jnp.where(lane == domains[b], picked, 0.0)
        start_losses(0, tile)

    def turn_targets():
        def turn(g, carry):
            t_copy(g).wait()
            for b in range(2):
                for h in range(per_group):
                    columns = pl.ds(pl.multiple_of(g * heads_w + h * HD, HD), HD)
                    tT[g, b, :, HD * h : HD * (h + 1)] = tv[BLOCK * b : BLOCK * (b + 1), columns].T
            return carry

        lax.fori_loop(0, groups, turn, 0)

    def columns(g, h):
        return pl.ds(pl.multiple_of(g * heads_w + h * HD, HD), HD)

    def queries_of(g, b):
        first = BLOCK * b
        return jnp.concatenate([qv[first : first + BLOCK, columns(g, h)] for h in range(per_group)], 0)

    def forward(g, slot):
        @pl.when(g == 0)
        def _():
            for i in (0, 3, 4):
                halo_copy(0, i).wait_recv()

        @pl.when(g > 0)
        def _():
            halo_copy(g, 2).wait_recv()
            halo_copy(g, 3).wait_recv()

        q_copy(g).wait()
        kT[slot] = kv[g, 0].T
        vT[...] = kv[g, 1].T
        for b in range(2):
            first = BLOCK * b
            scores = dot(kv[g, 0, first : first + WINDOW, :], queries_of(g, b), NT)
            parts, top = [], None
            for j in range(MOST):
                part = scores[BLOCK * j : BLOCK * (j + 1)]
                if j == MOST - 1:
                    part = part + tri[...]
                parts.append(part)
                part_top = jnp.max(part.reshape(BLOCK // 8, 8, heads_w), axis=0)
                if j < MOST - 1:
                    part_top = part_top + bias[b][j]
                top = part_top if top is None else jnp.maximum(top, part_top)
            shift = jnp.max(top, axis=0, keepdims=True) * (SCALE * LOG2E)
            raised_low, sums = [], None
            for j in range(MOST):
                off = shift if j == MOST - 1 else shift - bias[b][j]
                part = jnp.exp2(parts[j] * (SCALE * LOG2E) - off)
                raised_low.append(part.astype(bf16))
                part_sum = jnp.sum(part.reshape(BLOCK // 8, 8, heads_w), axis=0)
                sums = part_sum if sums is None else sums + part_sum
            inverse = 1.0 / jnp.sum(sums, axis=0, keepdims=True)
            raised_low = jnp.concatenate(raised_low, 0)
            raised[slot, b] = raised_low
            out = dot(vT[:, first : first + WINDOW], raised_low, NN) * inverse
            error = out - tT[g, b].astype(f32)
            squares = error * error
            lossv[b] += jnp.sum(squares.reshape(HD // 8, 8, heads_w), axis=0)
            grad_out = (error * (inverse * omegas[b])).astype(bf16)
            gout[slot, b] = grad_out
            center[slot, b] = jnp.sum(grad_out.astype(f32) * out, axis=0, keepdims=True)

    def backward(g, slot, between):
        grad_scores = []
        for b in range(2):
            first = BLOCK * b
            grad_out = gout[slot, b]
            grad_probs = dot(kv[g, 1, first : first + WINDOW, :], grad_out, NN)
            grad_score = (raised[slot, b].astype(f32) * (grad_probs - center[slot, b])).astype(bf16)
            grad_scores.append(grad_score)
            grad_value = dot(raised[slot, b], grad_out, NT)
            grad_key = dot(grad_score, queries_of(g, b), NN) * SCALE
            for which, part in ((0, grad_key), (1, grad_value)):
                if b == 0:
                    acc[which, 0:WINDOW, :] = part
                else:
                    acc[which, BLOCK:WINDOW, :] += part[0 : WINDOW - BLOCK]
                    acc[which, WINDOW:, :] = part[WINDOW - BLOCK :]
        between()
        send_grads(g)
        for b in range(2):
            first = BLOCK * b
            grad_query = dot(kT[slot, :, first : first + WINDOW], grad_scores[b], NN) * SCALE
            for h in range(per_group):
                gq_ref[first : first + BLOCK, columns(g, h)] = grad_query[:, HD * h : HD * (h + 1)].T.astype(bf16)

    def first_groups(g, carry):
        forward(g, 0)

        @pl.when(g == 0)
        def _():
            relay_halo(1)
            send_halo(2)
            send_halo(3)

        @pl.when(g == 1)
        def _():
            relay_halo(2)
            relay_halo(3)

        def between():
            @pl.when(g == 1)
            def _():
                relay_grads(0)

        backward(g, 0, between)
        return carry

    def last_forward(i, carry):
        forward(2 + i, i)
        return carry

    def last_backward(i, carry):
        def between():
            @pl.when(i == 0)
            def _():
                finish(0)

            @pl.when(i == 1)
            def _():
                start_losses(1, add_losses(0))

        backward(2 + i, i, between)
        return carry

    pl.semaphore_wait(barrier, n_ctx - 1 + n_dp - 1)
    send_halo(0)
    halo_copy(0, 4).start()
    send_halo(1)
    turn_targets()
    halo_copy(0, 1).wait_recv()
    halo_copy(0, 3).start()
    lax.fori_loop(0, 2, first_groups, 0)
    lax.fori_loop(0, 2, last_forward, 0)
    slab_losses()
    relay_grads(1)
    lax.fori_loop(0, 2, last_backward, 0)
    relay_grads(2)
    finish(1)
    relay_grads(3)
    finish(2)
    finish(3)
    tile = add_losses(1)
    loss_ref[...] = tile[0:1] / (jnp.maximum(tile[1:2], 1.0) * float(groups * per_group * HD))
    for g in range(groups):
        for i in (0, 1, 3, 4) if g == 0 else (0, 1, 2, 3):
            halo_copy(g, i).wait_send()
        for i in range(5):
            grad_copy(g, i).wait_send()


def write(gq_ref, gk_ref, gv_ref, loss_ref, gq_hbm, gk_hbm, gv_hbm, loss_out, sems):
    pairs = ((gq_ref, gq_hbm), (gk_ref, gk_hbm), (gv_ref, gv_hbm))
    copies = [pltpu.make_async_copy(src, dst, sems.at[i]) for i, (src, dst) in enumerate(pairs)]
    for copy in copies:
        copy.start()
    loss_out[...] = loss_ref[0, 0:DOMAINS]
    for copy in copies:
        copy.wait()


def on_device(n_ctx, n_dp, queries, key_states, value_states, targets, doc_blocks, doc_domain, domain_weight):
    rows, q_width = queries.shape[1:]
    kv_width = key_states.shape[2]
    groups = kv_width // HD
    per_group = q_width // kv_width
    heads_w = per_group * HD
    any_space = pl.BlockSpec(memory_space=pl.ANY)
    smem = pl.BlockSpec(memory_space=pltpu.SMEM)
    vmem = pl.BlockSpec(memory_space=pltpu.VMEM)
    dma = pltpu.SemaphoreType.DMA
    span = HALO + rows
    most_peers = max(n_ctx, n_dp)
    gq, gk, gv, loss = pl.pallas_call(
        functools.partial(kernel, n_ctx, n_dp, groups, per_group),
        out_shape=(
            pltpu.VMEM((rows, q_width), bf16),
            pltpu.VMEM((rows, kv_width), bf16),
            pltpu.VMEM((rows, kv_width), bf16),
            pltpu.VMEM((1, HD), f32),
        ),
        in_specs=[smem, smem, smem, any_space, any_space, any_space, any_space],
        out_specs=(vmem,) * 4,
        scratch_shapes=[
            pltpu.VMEM((rows, q_width), bf16),
            pltpu.VMEM((rows, q_width), bf16),
            pltpu.VMEM((groups, 2, HD, heads_w), bf16),
            pltpu.VMEM((groups, 2, span, HD), bf16),
            pltpu.VMEM((2, HD, span), bf16),
            pltpu.VMEM((HD, span), bf16),
            pltpu.VMEM((2, 2, WINDOW, heads_w), bf16),
            pltpu.VMEM((2, 2, HD, heads_w), bf16),
            pltpu.VMEM((2, 2, 1, heads_w), f32),
            pltpu.VMEM((2, span, HD), f32),
            pltpu.VMEM((groups, 2, rows, HD), f32),
            pltpu.VMEM((2, 2, 2, BLOCK, HD), f32),
            pltpu.VMEM((groups, 5, 2, BLOCK, HD), bf16),
            pltpu.VMEM((groups, 5, 2, BLOCK, HD), bf16),
            pltpu.VMEM((2, 8, heads_w), f32),
            pltpu.VMEM((2, 8, HD), f32),
            pltpu.VMEM((2, most_peers, 8, HD), f32),
            pltpu.VMEM((BLOCK, heads_w), f32),
            dma((groups, 2)),
            dma((groups,)),
            dma((groups,)),
            dma((groups, 5)),
            dma((groups, 5)),
            dma((groups, 5)),
            dma((groups, 5)),
            dma((2, most_peers)),
            dma((2, most_peers)),
        ],
        compiler_params=pltpu.CompilerParams(collective_id=0, has_side_effects=True, vmem_limit_bytes=56 << 20),
    )(doc_blocks, doc_domain, domain_weight, queries[0], key_states[0], value_states[0], targets[0])
    gq, gk, gv, loss = pl.pallas_call(
        write,
        out_shape=(
            jax.ShapeDtypeStruct((rows, q_width), bf16),
            jax.ShapeDtypeStruct((rows, kv_width), bf16),
            jax.ShapeDtypeStruct((rows, kv_width), bf16),
            jax.ShapeDtypeStruct((DOMAINS,), f32),
        ),
        in_specs=[vmem] * 4,
        out_specs=(any_space, any_space, any_space, vmem),
        scratch_shapes=[dma((3,))],
    )(*(pltpu.with_memory_space_constraint(x, pltpu.VMEM) for x in (gq, gk, gv, loss)))
    return gq[None], gk[None], gv[None], loss


def solution(mesh):
    placed = (
        P("dp", "ctx", None),
        P("dp", "ctx", None),
        P("dp", "ctx", None),
        P("dp", "ctx", None),
        P("dp", None),
        P("dp", None),
        P(),
    )
    return jax.shard_map(
        functools.partial(on_device, mesh.shape["ctx"], mesh.shape["dp"]),
        mesh=mesh,
        in_specs=placed,
        out_specs=(P("dp", "ctx", None), P("dp", "ctx", None), P("dp", "ctx", None), P()),
        check_vma=False,
    )
```
